32 devices in a mesh: grp: 2 (over y), cuts: 4 (over z), space: 4 (over x, core).
Axes of the slice: x: 2, y: 2, z: 4, core: 2. Of those that a mesh axis runs over, the one named last changes fastest.
Arguments:
- left_modes: float32 [8, 1024, 1024], P(('grp', 'cuts'), None, 'space'), parts along dimension 0, may hold values from -0.25 to 0.25
- right_modes: float32 [8, 1024, 1024], P(('grp', 'cuts'), None, 'space'), parts along dimension 0, may hold values from -6 to 6
- momenta: int32 [4, 3], replicated, may hold values from -2 to 2
- partners: int32 [4], replicated, may hold values from 0 to 3, as said below
Outputs:
- meson_field: float32 [8, 1024, 4, 1024], P(('grp', 'cuts'), 'space'), parts along dimension 0
- product: float32 [8, 1024, 4, 1024], P(('grp', 'cuts'), 'space'), parts along dimension 0
The draws below stay inside these ranges and needn't reach their ends.
There are 2 independent parts, one for each index of `grp`. The reference program is written for one: setup_inputs(seed, part) draws one part's arguments, and reference() takes and returns one part's arrays. A program takes and returns all parts, laid end to end along the dimension named above; an argument that names none is the same for every part. Nothing has to cross between parts.
Inputs may be any that keep to these rules, and one draw needn't show every extreme that they name: `partners`: every slice is named exactly once.
All inputs are finite; a program needn't handle non-finite values.
Results may differ from the reference program's by a relative error of at most 0.00011.
Values sent between devices are 32-bit elements; how exact they have to be, the bound alone decides.
No kernel may reach another device: no remote copies, remote signals or barrier semaphores. Data moves between devices by JAX's collectives and lax.ppermute only.
A program may use at most 64 MiB of HBM per device.

```python
import math
import jax
import jax.numpy as jnp
from jax import lax

MODES = 1024
VERTS = 4
NT = 4
SITES = 1024


def force_entry(table, where, target):
    holder = jnp.argmax((table == target).astype(jnp.int32)).astype(jnp.int32)
    before = table[where]
    table = table.at[holder].set(before)
    return table.at[where].set(target)


def draw_partners(key, part):
    order_key = jax.random.fold_in(key, 11)
    pick_key = jax.random.fold_in(key, 12)
    table = jax.random.permutation(order_key, NT).astype(jnp.int32)
    chosen = jax.random.randint(pick_key, (), 0, NT).astype(jnp.int32)
    table = force_entry(table, chosen, (chosen + NT - 1) % NT)
    second = (chosen + 1) % NT
    table = force_entry(table, second, (second + NT // 2) % NT)
    return table.astype(jnp.int32)


def touch_ends(result, own_key, smallest, top_value):
    longest = result.shape.index(max(result.shape))
    spots = []
    for shift in (0, 1):
        where = [jax.random.randint(jax.random.fold_in(own_key, axis), (), 0, length) for axis, length in enumerate(result.shape)]
        where[longest] = (where[longest] + shift) % result.shape[longest]
        spots.append(tuple(where))
    return result.at[spots[0]].set(smallest).at[spots[1]].set(top_value)


def raised(result, stream_key, source, target, parts, factor):
    owner, partner = [(jnp.arange(result.shape[axis_at]) // (result.shape[axis_at] // parts)).reshape([-1 if axis == axis_at else 1 for axis in range(result.ndim)]) for axis_at in (source, target)]
    chosen = jax.random.permutation(stream_key, parts)[partner]
    strong = (owner == chosen) | (owner == (partner + parts // 2) % parts)
    return jnp.where(strong, factor * result, result)


def steps_of(own_key, extent, pieces, smallest, top_value):
    loudness, own = 1.0, jax.random.fold_in(own_key, 6)
    for position, shards_of in pieces:
        heights = jnp.exp(jax.random.uniform(jax.random.fold_in(own, position), (shards_of,), jnp.float32, smallest / len(pieces), top_value / len(pieces)))
        loudness = loudness * jnp.repeat(heights, extent[position] // shards_of).reshape([-1 if axis == position else 1 for axis in range(len(extent))])
    return loudness


def normal_values(rng, extent, spread, bound, pieces=(), held_as=jnp.bfloat16):
    factor_of = steps_of(rng, extent, pieces, -0.22, 0.18) if pieces else 1.0
    drawn = jax.random.normal(rng, extent, jnp.float32) * spread * factor_of
    return jnp.minimum(jnp.maximum(drawn, -bound), bound).astype(held_as)


def noise_with(key, shape, scale, limit, cuts, heavy, kind=jnp.bfloat16):
    drawn = scale * jax.random.normal(key, shape, jnp.float32)
    if cuts:
        drawn = drawn * steps_of(key, shape, cuts, -0.22, 0.18)
    return jnp.clip(raised(drawn, jax.random.fold_in(key, 3), *heavy), -limit, limit).astype(kind)


def setup_inputs(seed: int = 0, part: int = 0) -> dict:
    seeds = jax.random.split(jax.random.key(seed), 5)
    part_splits = jax.random.split(jax.random.fold_in(seeds[4], part), 5)
    return {
        "left_modes": noise_with(part_splits[0], (NT, MODES, SITES), SITES ** -0.5, 0.25, ((0, 4), (2, 4)), (2, 1, 4, 2.0), jnp.float32),
        "right_modes": normal_values(part_splits[1], (NT, MODES, SITES), 1.0, 6.0, ((0, 4), (2, 4)), jnp.float32),
        "momenta": touch_ends(jax.random.randint(seeds[2], (VERTS, 3), -2, 3), jax.random.fold_in(seeds[2], 1), -2, 2).astype(jnp.int32),
        "partners": draw_partners(jax.random.fold_in(seeds[4], 71), part),
    }


def phase_table(momenta, offset, amount, site_total):
    global_site = offset + jnp.arange(amount, dtype=jnp.int32)
    coord_x = global_site % 8
    coord_y = global_site // 8 % 8
    coord_z = global_site // 64
    depth = site_total // 64
    numerator = ((momenta[:, 0:1] * coord_x[None] + momenta[:, 1:2] * coord_y[None]) * depth + momenta[:, 2:3] * coord_z[None] * 8) % (8 * depth)
    return jnp.cos(2.0 * math.pi * numerator.astype(jnp.float32) / (8 * depth))

def reference(left_modes, right_modes, momenta, partners):
    phases = phase_table(momenta, jnp.int32(0), SITES, SITES)

    def one_slice(index):
        weighted = left_modes[index][:, None, :] * phases[None]
        return jnp.einsum('max,nx->man', weighted, right_modes[index], precision=lax.Precision.HIGHEST)
    meson_field = lax.map(one_slice, jnp.arange(NT, dtype=jnp.int32))
    first_vertex = meson_field[partners][:, :, 0, :]
    product = jnp.einsum('tmak,tkn->tman', meson_field, first_vertex, precision=lax.Precision.HIGHEST) * (1.0 / math.sqrt(MODES))
    return (meson_field, product)
```

```python
import functools
import math

import jax
import jax.numpy as jnp
from jax import lax
from jax.experimental import pallas as pl
from jax.experimental.pallas import tpu as pltpu
from jax.sharding import PartitionSpec as P

LANES = 128
VMEM = pl.BlockSpec(memory_space=pltpu.VMEM)
VMEM_LIMIT = 60 * 2**20


def partner(value, axis, bit):
    mask = 2**bit
    pairs = [(source, source ^ mask) for source in range(lax.axis_size(axis))]
    return lax.ppermute(value, axis, pairs)


def phase_table(momenta, offset, amount, site_total):
    global_site = offset + jnp.arange(amount, dtype=jnp.int32)
    coord_x = global_site % 8
    coord_y = global_site // 8 % 8
    coord_z = global_site // 64
    depth = site_total // 64
    numerator = (
        (momenta[:, 0:1] * coord_x[None] + momenta[:, 1:2] * coord_y[None]) * depth
        + momenta[:, 2:3] * coord_z[None] * 8
    ) % (8 * depth)
    return jnp.cos(2.0 * math.pi * numerator.astype(jnp.float32) / (8 * depth))


def split(value):
    high = value.astype(jnp.bfloat16)
    low = (value - high.astype(jnp.float32)).astype(jnp.bfloat16)
    return high, low


def dot3(a_high, a_low, b_high, b_low, dims):
    dot = functools.partial(
        lax.dot_general, dimension_numbers=(dims, ((), ())), preferred_element_type=jnp.float32
    )
    return dot(a_high, b_high) + (dot(a_high, b_low) + dot(a_low, b_high))


def weigh_kernel(count, width, *refs):
    lefts, phase, high, low = refs[:count], refs[count], refs[count + 1], refs[count + 2]
    for piece in range(count):
        here = slice(piece * width, (piece + 1) * width)
        value = lefts[piece][...]
        for vertex in range(phase.shape[0]):
            weighted = value * phase[vertex : vertex + 1, here]
            high[vertex, :, here], low[vertex, :, here] = split(weighted)


def weigh(lefts, phase):
    count, (rows, width) = len(lefts), lefts[0].shape
    shape = jax.ShapeDtypeStruct((phase.shape[0], rows, count * width), jnp.bfloat16)
    return pl.pallas_call(
        functools.partial(weigh_kernel, count, width),
        out_shape=(shape, shape),
        in_specs=[VMEM] * (count + 1),
        out_specs=(VMEM, VMEM),
        compiler_params=pltpu.CompilerParams(vmem_limit_bytes=VMEM_LIMIT),
        name="weigh",
    )(*lefts, phase)


def first_kernel(count, width, *refs):
    rights, (high, low, out) = refs[:count], refs[count:]
    total = None
    for piece in range(count):
        here = slice(piece * width, (piece + 1) * width)
        right_high, right_low = split(rights[piece][...])
        term = dot3(high[0, :, here], low[0, :, here], right_high, right_low, ((1,), (1,)))
        total = term if total is None else total + term
    out[...] = total


def first_field(high, low, rights):
    count, (columns, width) = len(rights), rights[0].shape
    vertices, rows, sites = high.shape
    one = pl.BlockSpec((1, rows, sites), lambda step: (0, 0, 0))
    whole = pl.BlockSpec((columns, width), lambda step: (0, 0))
    return pl.pallas_call(
        functools.partial(first_kernel, count, width),
        grid=(1,),
        out_shape=jax.ShapeDtypeStruct((rows, columns), jnp.float32),
        in_specs=[whole] * count + [one, one],
        out_specs=pl.BlockSpec((rows, columns), lambda step: (0, 0)),
        compiler_params=pltpu.CompilerParams(vmem_limit_bytes=VMEM_LIMIT),
        name="first",
    )(*rights, high, low)


def store_tiles(out, first_tile, vertex, value):
    for tile in range(value.shape[1] // LANES):
        out[:, first_tile + tile, vertex, :] = value[:, tile * LANES : (tile + 1) * LANES]


def field_kernel(pieces, widths, width, *refs):
    chunks = len(widths)
    rights, refs = refs[: chunks * pieces], refs[chunks * pieces :]
    firsts, (high, low, out, field_high, field_low) = refs[:chunks], refs[chunks:]
    vertices, rows, _ = high.shape
    begin = 0
    for chunk in range(chunks):
        end = begin + widths[chunk]
        totals = [firsts[chunk][...]]
        halves = [split(ref[...]) for ref in rights[chunk * pieces : (chunk + 1) * pieces]]
        for vertex in range(1, vertices):
            total = None
            for piece in range(pieces):
                here = slice(piece * width, (piece + 1) * width)
                term = dot3(
                    high[vertex, :, here], low[vertex, :, here], *halves[piece], ((1,), (1,))
                )
                total = term if total is None else total + term
            totals.append(total)
        for vertex in range(vertices):
            store_tiles(out, begin // LANES, vertex, totals[vertex])
            parts = split(totals[vertex])
            field_high[vertex, :, begin:end], field_low[vertex, :, begin:end] = parts
        begin = end


def whole_field(high, low, rights, firsts):
    pieces, width = len(rights[0]), rights[0][0].shape[1]
    widths = tuple(first.shape[1] for first in firsts)
    vertices, rows, _ = high.shape
    modes = sum(widths)
    flat = [right for chunk in rights for right in chunk]
    part = jax.ShapeDtypeStruct((vertices, rows, modes), jnp.bfloat16)
    return pl.pallas_call(
        functools.partial(field_kernel, pieces, widths, width),
        out_shape=(
            jax.ShapeDtypeStruct((rows, modes // LANES, vertices, LANES), jnp.float32),
            part,
            part,
        ),
        in_specs=[VMEM] * (len(flat) + len(firsts) + 2),
        out_specs=(VMEM,) * 3,
        compiler_params=pltpu.CompilerParams(vmem_limit_bytes=VMEM_LIMIT),
        name="field",
    )(*flat, *firsts, high, low)


def product_kernel(count, scale, place, high, low, *refs):
    pieces, refs = refs[:count], refs[count:]
    out, second_high, second_low = refs[-3:]
    rows = pieces[0].shape[0]
    vertices, height, modes = high.shape

    @pl.when(pl.program_id(0) == 0)
    def _():
        for piece in range(count):
            here = pl.ds(pl.multiple_of(place[piece] * rows, rows), rows)
            second_high[here, :], second_low[here, :] = split(pieces[piece][...])

    total = dot3(
        high[...].reshape(vertices * height, modes),
        low[...].reshape(vertices * height, modes),
        second_high[...],
        second_low[...],
        ((1,), (0,)),
    )
    for vertex in range(vertices):
        store_tiles(out, 0, vertex, total[vertex * height : (vertex + 1) * height] * scale)


def product_chunk(buffer, begin, high, low, pieces, place, steps=4):
    count, (rows, columns) = len(pieces), pieces[0].shape
    vertices, _, modes = high.shape
    height = rows // steps
    tiles = columns // LANES
    field = pl.BlockSpec((vertices, height, modes), lambda step: (0, step, 0))
    whole = pl.BlockSpec((rows, columns), lambda step: (0, 0))
    any_space = pl.BlockSpec(memory_space=pl.ANY)
    aliased = [] if buffer is None else [buffer]
    return pl.pallas_call(
        functools.partial(product_kernel, count, 1.0 / math.sqrt(modes)),
        grid=(steps,),
        out_shape=jax.ShapeDtypeStruct((rows, modes // LANES, vertices, LANES), jnp.float32),
        in_specs=[pl.BlockSpec(memory_space=pltpu.SMEM), field, field]
        + [whole] * count
        + [any_space] * len(aliased),
        out_specs=pl.BlockSpec(
            (height, tiles, vertices, LANES), lambda step: (step, begin // columns, 0, 0)
        ),
        scratch_shapes=[pltpu.VMEM((modes, columns), jnp.bfloat16)] * 2,
        input_output_aliases={3 + count: 0} if aliased else {},
        compiler_params=pltpu.CompilerParams(vmem_limit_bytes=VMEM_LIMIT),
        name="product",
    )(place, high, low, *pieces, *aliased)


def from_partner(first, partners, slice_index):
    size = lax.axis_size("cuts")
    wanted = partners[slice_index]
    if size != 4:
        every = lax.all_gather(first, "cuts", axis=0)
        return lax.dynamic_index_in_dim(every, wanted, 0, keepdims=False)
    far = partner(first, "cuts", 1)
    passed_on = jnp.where(partners[slice_index ^ 1] == slice_index, first, far)
    near = partner(passed_on, "cuts", 0)
    return jnp.where(
        wanted == slice_index, first, jnp.where(wanted == (slice_index ^ 2), far, near)
    )


def chunk_widths(modes):
    if modes == 1024:
        return (128, 128, 256, 256, 128, 128)
    return (modes // 4,) * 4


def on_device(left_modes, right_modes, momenta, partners):
    left_local = left_modes[0]
    right_local = right_modes[0]
    modes, site_local = left_local.shape
    space_size = lax.axis_size("space")
    site_total = site_local * space_size
    rows = modes // space_size
    bits = space_size.bit_length() - 1
    space_index = lax.axis_index("space")
    slice_index = lax.axis_index("cuts")
    widths = chunk_widths(modes)
    begins = [sum(widths[:chunk]) for chunk in range(len(widths))]

    blocks = left_local.reshape(space_size, rows, site_local)
    items = {
        (to_go, 0): lax.dynamic_index_in_dim(blocks, space_index ^ to_go, 0, keepdims=False)
        for to_go in range(space_size)
    }
    rights = [
        {0: right_local[begin : begin + width]} for begin, width in zip(begins, widths)
    ]
    for bit in range(bits - 1, -1, -1):
        mask = 2**bit
        sent = [key for key in items if key[0] & mask]
        for come in sorted({key[1] for key in sent}):
            keys = [key for key in sent if key[1] == come]
            if len(keys) > 1:
                received = partner(jnp.stack([items.pop(key) for key in keys]), "space", bit)
                received = [received[place] for place in range(len(keys))]
            else:
                received = [partner(items.pop(keys[0]), "space", bit)]
            for key, value in zip(keys, received):
                items[(key[0] ^ mask, key[1] ^ mask)] = value
    offsets = [0]
    for bit in range(bits - 1, -1, -1):
        offsets = offsets + [offset ^ 2**bit for offset in offsets]
    phase = jnp.concatenate(
        [
            phase_table(momenta, (space_index ^ offset) * site_local, site_local, site_total)
            for offset in offsets
        ],
        axis=1,
    )
    high, low = weigh([items[(0, offset)] for offset in offsets], phase)

    def gathered(own):
        pieces = [own]
        for bit in range(bits - 1, -1, -1):
            pieces = pieces + [partner(piece, "space", bit) for piece in pieces]
        return pieces

    all_rights = [gathered(right[0]) for right in rights]
    firsts = [first_field(high, low, pieces) for pieces in all_rights]
    seconds = [gathered(from_partner(first, partners, slice_index)) for first in firsts]
    meson, field_high, field_low = whole_field(high, low, all_rights, firsts)
    place = jnp.stack([space_index ^ offset for offset in offsets]).astype(jnp.int32)
    product = None
    for begin, pieces in zip(begins, seconds):
        product = product_chunk(product, begin, field_high, field_low, pieces, place)

    def whole(tiles):
        return tiles.transpose(0, 2, 1, 3).reshape(1, rows, momenta.shape[0], modes)

    return (whole(meson), whole(product))


def solution(mesh):
    in_specs = (P(("grp", "cuts"), None, "space"), P(("grp", "cuts"), None, "space"), P(), P())
    out_specs = (P(("grp", "cuts"), "space", None, None), P(("grp", "cuts"), "space", None, None))
    return jax.shard_map(
        on_device, mesh=mesh, in_specs=in_specs, out_specs=out_specs, check_vma=False
    )
```
